32 devices in a mesh: groups: 2 (over x), ctx: 16 (over z, y, core).
Axes of the slice: x: 2, y: 2, z: 4, core: 2. Of those that a mesh axis runs over, the one named last changes fastest.
Arguments:
- queries: bfloat16 [4096, 4096], P(('groups', 'ctx')), parts along dimension 0, may hold values from -130 to 130
- keys_values: bfloat16 [4096, 1024], P(('groups', 'ctx')), parts along dimension 0, may hold values from -25 to 25
- out_grad: bfloat16 [4096, 4096], P(('groups', 'ctx')), parts along dimension 0, may hold values from -6 to 6
- key_blocks: int32 [32, 3], P('groups'), parts along dimension 0, may hold values from 0 to 15, as said below
- key_count: int32 [32], P('groups'), parts along dimension 0, may hold values from 1 to 3, as said below
- block_at_slot: int32 [32], P('groups'), parts along dimension 0, may hold values from 0 to 15, as said below
Outputs:
- attended: bfloat16 [4096, 4096], P(('groups', 'ctx')), parts along dimension 0
- query_grad: bfloat16 [4096, 4096], P(('groups', 'ctx')), parts along dimension 0
- kv_grad: bfloat16 [4096, 1024], P(('groups', 'ctx')), parts along dimension 0
The draws below stay inside these ranges and needn't reach their ends.
There are 2 independent parts, one for each index of `groups`. The reference program is written for one: setup_inputs(seed, part) draws one part's arguments, and reference() takes and returns one part's arrays. A program takes and returns all parts, laid end to end along the dimension named above; each array names one. Nothing has to cross between parts.
Inputs may be any that keep to these rules, and one draw needn't show every extreme that they name: `block_at_slot`: A permutation of the block ids. `key_blocks`: each row lists 3 distinct block ids, the first being the row's own block. Every listed block sits at most 2 slots away from the row's block in the layout of block_at_slot, and some live entry sits exactly 2 slots away. `key_count`: some row has 3 live entries.
All inputs are finite; a program needn't handle non-finite values.
Results may differ from the reference program's by a relative error of at most 0.02.
Values may be sent and summed in bfloat16 or wider, within the bound.
A program may use at most 128 MiB of HBM per device.

```python
import jax
import jax.numpy as jnp
from jax import lax

HEADS = 32
KV_HEADS = 4
HEAD = 128
BLOCK = 128
REACH = 2
KOTH = 2
KMAX = 3
NB = 16
TOKENS = 2048


def mask_tables(key):
    order = jax.random.permutation(jax.random.fold_in(key, 7), NB).astype(jnp.int32)
    slots = jnp.arange(NB, dtype=jnp.int32)
    offsets = jnp.concatenate([jnp.arange(-REACH, 0), jnp.arange(1, REACH + 1)]).astype(jnp.int32)
    targets = slots[:, None] + offsets[None, :]
    inside = (targets >= 0) & (targets < NB)
    raw_scores = jax.random.randint(jax.random.fold_in(key, 8), (NB, 2 * REACH), 0, 1 << 20)
    ranked = raw_scores * (2 * REACH) + jnp.arange(2 * REACH, dtype=jnp.int32)[None, :]
    preferred = jnp.where(slots < NB // 2, REACH, -REACH)
    boosted = (slots[:, None] % 3 == 0) & (offsets[None, :] == preferred[:, None])
    ranked = jnp.where(boosted, ranked + (1 << 26), ranked)
    ranked = jnp.where(inside, ranked, -1)
    unused_top, picked = lax.top_k(ranked, KOTH)
    chosen = jnp.take_along_axis(targets, picked, axis=1)
    slot_lists = jnp.concatenate([slots[:, None], chosen], axis=1).astype(jnp.int32)
    light = jax.random.randint(jax.random.fold_in(key, 9), (NB,), 0, 2)
    heavy = (jax.random.randint(jax.random.fold_in(key, 10), (NB,), 0, 4) == 0).astype(jnp.int32) * (KOTH - 1)
    others = light + heavy
    others = jnp.where(slots % 3 == 0, jnp.maximum(others, 1), others)
    others = jnp.where(slots == 0, KOTH, others)
    table = order[slot_lists]
    block_lists = jnp.zeros((NB, KMAX), jnp.int32).at[order].set(table)
    counts = jnp.zeros((NB,), jnp.int32).at[order].set(1 + others)
    return (block_lists, counts.astype(jnp.int32), order)


def attention_draws(key):
    heads_width = HEADS * HEAD
    pair_width = KV_HEADS * HEAD
    query_part = jnp.clip(jax.random.normal(jax.random.fold_in(key, 21), (TOKENS, heads_width), jnp.float32), -6.0, 6.0)
    key_part = jnp.clip(jax.random.normal(jax.random.fold_in(key, 22), (TOKENS, pair_width), jnp.float32), -6.0, 6.0)
    value_part = jnp.clip(jax.random.normal(jax.random.fold_in(key, 23), (TOKENS, pair_width), jnp.float32), -6.0, 6.0)
    return (query_part, jnp.concatenate([key_part, value_part], axis=1))


def draw_queries(key, part):
    return attention_draws(key)[0].astype(jnp.bfloat16)


def draw_keys_values(key, part):
    return attention_draws(key)[1].astype(jnp.bfloat16)


def draw_key_blocks(key, part):
    return mask_tables(key)[0]


def draw_key_count(key, part):
    return mask_tables(key)[1]


def draw_block_at_slot(key, part):
    return mask_tables(key)[2]


def levels(key, dims, cuts, smallest, top_value):
    def one(position, shards_of):
        steps = jax.random.uniform(jax.random.fold_in(jax.random.fold_in(key, 6), position), (shards_of,), jnp.float32, smallest / len(cuts), top_value / len(cuts))
        return jnp.repeat(jnp.exp(steps), dims[position] // shards_of).reshape((-1,) + (1,) * (len(dims) - position - 1))

    factor_of = one(*cuts[0])
    for cut in cuts[1:]:
        factor_of = factor_of * one(*cut)
    return factor_of


def gaussian(rng, shape, scale, limit, cuts=(), held_as=jnp.bfloat16):
    drawn = scale * jax.random.normal(rng, shape, jnp.float32)
    if cuts:
        drawn = drawn * levels(rng, shape, cuts, -0.22, 0.18)
    return jnp.clip(drawn, -limit, limit).astype(held_as)


def setup_inputs(seed: int = 0, part: int = 0) -> dict:
    arg_keys = jax.random.split(jax.random.key(seed), 7)
    own_keys = jax.random.split(jax.random.fold_in(arg_keys[6], part), 7)
    return {
        "queries": draw_queries(jax.random.fold_in(jax.random.fold_in(arg_keys[6], part), 71), part),
        "keys_values": draw_keys_values(jax.random.fold_in(jax.random.fold_in(arg_keys[6], part), 71), part),
        "out_grad": gaussian(own_keys[2], (TOKENS, HEADS * HEAD), 1.0, 6.0, ((0, 16),)),
        "key_blocks": draw_key_blocks(jax.random.fold_in(jax.random.fold_in(arg_keys[6], part), 71), part),
        "key_count": draw_key_count(jax.random.fold_in(jax.random.fold_in(arg_keys[6], part), 71), part),
        "block_at_slot": draw_block_at_slot(jax.random.fold_in(jax.random.fold_in(arg_keys[6], part), 71), part),
    }


def reference(queries, keys_values, out_grad, key_blocks, key_count, block_at_slot):
    block_count = block_at_slot.shape[0]
    tok_rows = BLOCK
    kv_width = keys_values.shape[1] // 2
    groups = kv_width // HEAD
    repeats = queries.shape[1] // kv_width
    score_scale = HEAD ** -0.5
    slot_range = jnp.arange(block_count, dtype=jnp.int32)
    slot_of_block = jnp.sum(jnp.where(block_at_slot[:, None] == slot_range[None, :], slot_range[:, None], 0), axis=0).astype(jnp.int32)
    row_blocks = key_blocks[block_at_slot]
    key_slots = slot_of_block[row_blocks].astype(jnp.int32)
    live_keys = jnp.arange(KMAX, dtype=jnp.int32)[None, :] < key_count[block_at_slot][:, None]
    query_blocks = queries.reshape(block_count, tok_rows, groups, repeats, HEAD).astype(jnp.float32)
    grad_blocks = out_grad.reshape(block_count, tok_rows, groups, repeats, HEAD).astype(jnp.float32)
    kv_blocks = keys_values.reshape(block_count, tok_rows, 2 * kv_width)

    def per_block(kv_total, inputs):
        query_heads, grad_heads, slots, live = inputs
        chosen = kv_blocks[slots].astype(jnp.float32)
        key_rows = chosen[:, :, :kv_width].reshape(KMAX * tok_rows, groups, HEAD)
        value_rows = chosen[:, :, kv_width:].reshape(KMAX * tok_rows, groups, HEAD)
        bias = jnp.repeat(jnp.where(live, 0.0, -1e30), tok_rows).astype(jnp.float32)
        scores = jnp.einsum("igrd,jgd->grij", query_heads, key_rows) * score_scale + bias
        best_score = jnp.max(scores, axis=-1)
        weights = jnp.exp(scores - best_score[..., None])
        weight_sum = jnp.sum(weights, axis=-1)
        rounded = lax.optimization_barrier(weights.astype(jnp.bfloat16)).astype(jnp.float32)
        mixed = jnp.einsum("grij,jgd->grid", rounded, value_rows) / weight_sum[..., None]
        out_heads = jnp.transpose(mixed, (2, 0, 1, 3)).astype(jnp.bfloat16)
        out_float = lax.optimization_barrier(out_heads).astype(jnp.float32)
        log_total = best_score + jnp.log(weight_sum)
        delta_rows = jnp.einsum("igrd,igrd->gri", grad_heads, out_float)
        probabilities = jnp.exp(scores - log_total[..., None])
        prob_grads = jnp.einsum("igrd,jgd->grij", grad_heads, value_rows)
        score_grads = probabilities * (prob_grads - delta_rows[..., None])
        grads_rounded = lax.optimization_barrier(score_grads.astype(jnp.bfloat16)).astype(jnp.float32)
        probs_rounded = lax.optimization_barrier(probabilities.astype(jnp.bfloat16)).astype(jnp.float32)
        query_term = jnp.einsum("grij,jgd->igrd", grads_rounded, key_rows) * score_scale
        key_term = jnp.einsum("grij,igrd->jgd", grads_rounded, query_heads) * score_scale
        value_term = jnp.einsum("grij,igrd->jgd", probs_rounded, grad_heads)
        kv_term = jnp.concatenate([key_term.reshape(KMAX, tok_rows, kv_width), value_term.reshape(KMAX, tok_rows, kv_width)], axis=2)
        kv_total = kv_total.at[slots].add(kv_term)
        return kv_total, (out_heads.reshape(tok_rows, -1), query_term.reshape(tok_rows, -1).astype(jnp.bfloat16))

    start_total = jnp.zeros((block_count, tok_rows, 2 * kv_width), jnp.float32)
    kv_total, outputs = lax.scan(per_block, start_total, (query_blocks, grad_blocks, key_slots, live_keys))
    attended = outputs[0].reshape(block_count * tok_rows, -1)
    query_grad = outputs[1].reshape(block_count * tok_rows, -1)
    kv_grad = kv_total.reshape(block_count * tok_rows, -1).astype(jnp.bfloat16)
    return (attended, query_grad, kv_grad)
```

```python
import functools

import jax
import jax.numpy as jnp
from jax import lax
from jax.experimental import pallas as pl
from jax.experimental.pallas import tpu as pltpu
from jax.sharding import PartitionSpec as P

HEAD = 128
OFFSETS = (-2, -1, 1, 2)
LOG2E = 1.4426950408889634
NEG = -1e30
NT = (((1,), (1,)), ((), ()))


def kernel(
    n, groups, repeats,
    blocks_ref, count_ref, slot_ref, q_hbm, kv_hbm, do_hbm,
    att_hbm, dq_hbm, kvg_hbm,
    q, kv, do, att, dq, kvg, near, own_grad, gsend, grecv,
    in_sem, kv_sem, out_sem, kvg_sem, near_send, near_recv, grad_send, grad_recv,
):
    rows = q.shape[0]
    wide = repeats * HEAD
    kv_width = groups * HEAD
    scale = HEAD ** (-0.5)
    me = lax.axis_index("ctx")

    def exists(o):
        return jnp.logical_and(me + OFFSETS[o] >= 0, me + OFFSETS[o] < n)

    def target(o):
        return {"ctx": me + OFFSETS[o]}

    def column(g, width):
        return pl.ds(pl.multiple_of(g * width, width), width)

    def near_copy(g, o, part):
        return pltpu.make_async_remote_copy(
            src_ref=kv_hbm.at[:, pl.ds(pl.multiple_of(part * kv_width + g * HEAD, HEAD), HEAD)],
            dst_ref=near.at[g, 3 - o, part],
            send_sem=near_send.at[g, o, part],
            recv_sem=near_recv.at[g, 3 - o, part],
            device_id=target(o),
            device_id_type=pl.DeviceIdType.MESH,
        )

    def grad_copy(g, o):
        return pltpu.make_async_remote_copy(
            src_ref=gsend.at[g, o],
            dst_ref=grecv.at[g, 3 - o],
            send_sem=grad_send.at[g, o],
            recv_sem=grad_recv.at[g, 3 - o],
            device_id=target(o),
            device_id_type=pl.DeviceIdType.MESH,
        )

    def load_copies(g):
        return (
            pltpu.make_async_copy(q_hbm.at[:, column(g, wide)], q.at[:, column(g, wide)], in_sem.at[g, 0]),
            pltpu.make_async_copy(do_hbm.at[:, column(g, wide)], do.at[:, column(g, wide)], in_sem.at[g, 1]),
        )

    def store_copies(g):
        return (
            pltpu.make_async_copy(att.at[:, column(g, wide)], att_hbm.at[:, column(g, wide)], out_sem.at[g, 0]),
            pltpu.make_async_copy(dq.at[:, column(g, wide)], dq_hbm.at[:, column(g, wide)], out_sem.at[g, 1]),
        )

    kv_load = pltpu.make_async_copy(kv_hbm, kv, kv_sem)

    barrier = pltpu.get_barrier_semaphore()
    arrivals = jnp.int32(0)
    for o in range(4):
        there = exists(o)
        arrivals = arrivals + there.astype(jnp.int32)

        @pl.when(there)
        def _():
            pl.semaphore_signal(barrier, inc=1, device_id=target(o), device_id_type=pl.DeviceIdType.MESH)

        @pl.when(jnp.logical_not(there))
        def _():
            near[:, o] = jnp.zeros((groups, 2, rows, HEAD), near.dtype)
            grecv[:, o] = jnp.zeros((groups, 2, rows, HEAD), grecv.dtype)

    kv_load.start()
    for g in range(groups):
        for copy in load_copies(g):
            copy.start()
    pl.semaphore_wait(barrier, arrivals)

    for g in range(groups):
        for o in (3, 0, 2, 1):

            @pl.when(exists(o))
            def _():
                near_copy(g, o, 0).start()
                near_copy(g, o, 1).start()

    own_block = slot_ref[me]
    live_count = count_ref[own_block]
    chosen = []
    bias = []
    for j in (1, 2):
        wanted = blocks_ref[own_block, j]
        hits = []
        for o in range(4):
            there = jnp.clip(me + OFFSETS[o], 0, n - 1)
            hits.append(exists(o) & (slot_ref[there] == wanted) & (live_count > j))
        chosen.append(hits)
        bias.append(jnp.where(hits[0] | hits[1] | hits[2] | hits[3], 0.0, NEG).astype(jnp.float32))

    kv_load.wait()

    def pick(g, part, hits):
        value = near[g, 0, part]
        for o in range(1, 4):
            value = jnp.where(hits[o], near[g, o, part], value)
        return value

    def step(g, carry):
        for copy in load_copies(g):
            copy.wait()
        for o in range(4):

            @pl.when(exists(3 - o))
            def _():
                near_copy(g, o, 0).wait_recv()
                near_copy(g, o, 1).wait_recv()

        own_key = kv[:, pl.ds(pl.multiple_of(g * HEAD, HEAD), HEAD)]
        own_value = kv[:, pl.ds(pl.multiple_of(kv_width + g * HEAD, HEAD), HEAD)]
        keys = jnp.concatenate([own_key, pick(g, 0, chosen[0]), pick(g, 0, chosen[1])], axis=0)
        values = jnp.concatenate([own_value, pick(g, 1, chosen[0]), pick(g, 1, chosen[1])], axis=0)
        keys_t = keys.T
        values_t = values.T
        key_grad = jnp.zeros((3 * rows, HEAD), jnp.float32)
        value_grad = jnp.zeros((3 * rows, HEAD), jnp.float32)
        for pair in range(repeats // 2):
            starts = [pl.multiple_of(g * wide + (2 * pair + i) * HEAD, HEAD) for i in range(2)]
            q2 = jnp.concatenate([q[:, pl.ds(s, HEAD)] for s in starts], axis=0)
            do2 = jnp.concatenate([do[:, pl.ds(s, HEAD)] for s in starts], axis=0)
            raw = lax.dot_general(keys, q2, NT, preferred_element_type=jnp.float32) * (scale * LOG2E)
            scores = jnp.concatenate(
                [raw[:rows], raw[rows : 2 * rows] + bias[0], raw[2 * rows :] + bias[1]], axis=0
            )
            best = jnp.max(scores, axis=0, keepdims=True)
            weights = jnp.exp2(scores - best)
            total = jnp.sum(weights, axis=0, keepdims=True)
            probs = weights * (1.0 / total)
            rounded = probs.astype(jnp.bfloat16)
            prob_grads = lax.dot_general(values, do2, NT, preferred_element_type=jnp.float32)
            delta = jnp.sum(probs * prob_grads, axis=0, keepdims=True)
            score_grads = (probs * (prob_grads - delta)).astype(jnp.bfloat16)
            mixed = jnp.dot(values_t, rounded, preferred_element_type=jnp.float32)
            query_grad = jnp.dot(keys_t, score_grads, preferred_element_type=jnp.float32) * scale
            mixed = mixed.astype(jnp.bfloat16).T
            query_grad = query_grad.astype(jnp.bfloat16).T
            for i in range(2):
                att[:, pl.ds(starts[i], HEAD)] = mixed[i * rows : (i + 1) * rows]
                dq[:, pl.ds(starts[i], HEAD)] = query_grad[i * rows : (i + 1) * rows]
            key_grad = key_grad + jnp.dot(score_grads, q2, preferred_element_type=jnp.float32)
            value_grad = value_grad + jnp.dot(rounded, do2, preferred_element_type=jnp.float32)
        for part, grad in ((0, key_grad * scale), (1, value_grad)):
            own_grad[g, part] = grad[:rows]
            for o in range(4):
                gsend[g, o, part] = jnp.where(
                    chosen[0][o], grad[rows : 2 * rows], jnp.where(chosen[1][o], grad[2 * rows :], 0.0)
                ).astype(jnp.bfloat16)
        for o in (3, 0, 2, 1):

            @pl.when(exists(o))
            def _():
                grad_copy(g, o).start()

        for copy in store_copies(g):
            copy.start()
        return carry

    lax.fori_loop(0, groups, step, 0)

    def finish(g, carry):
        for o in range(4):

            @pl.when(exists(3 - o))
            def _():
                grad_copy(g, o).wait_recv()

        for part in range(2):
            total = own_grad[g, part]
            for o in range(4):
                total = total + grecv[g, o, part].astype(jnp.float32)
            kvg[:, pl.ds(pl.multiple_of(part * kv_width + g * HEAD, HEAD), HEAD)] = total.astype(jnp.bfloat16)
        return carry

    lax.fori_loop(0, groups, finish, 0)
    kvg_store = pltpu.make_async_copy(kvg, kvg_hbm, kvg_sem)
    kvg_store.start()

    def drain(g, carry):
        for o in range(4):

            @pl.when(exists(o))
            def _():
                near_copy(g, o, 0).wait_send()
                near_copy(g, o, 1).wait_send()
                grad_copy(g, o).wait_send()

        for copy in store_copies(g):
            copy.wait()
        return carry

    lax.fori_loop(0, groups, drain, 0)
    kvg_store.wait()


def body(queries, keys_values, out_grad, key_blocks, key_count, block_at_slot):
    n = lax.axis_size("ctx")
    rows, width = queries.shape
    kv_width = keys_values.shape[1] // 2
    groups = kv_width // HEAD
    repeats = width // kv_width
    anywhere = pl.BlockSpec(memory_space=pl.ANY)
    scalars = pl.BlockSpec(memory_space=pltpu.SMEM)
    wide = pltpu.VMEM((rows, width), jnp.bfloat16)
    narrow = pltpu.VMEM((rows, 2 * kv_width), jnp.bfloat16)
    ring = pltpu.VMEM((groups, 4, 2, rows, HEAD), jnp.bfloat16)
    dma = pltpu.SemaphoreType.DMA
    return pl.pallas_call(
        functools.partial(kernel, n, groups, repeats),
        out_shape=(
            jax.ShapeDtypeStruct((rows, width), jnp.bfloat16),
            jax.ShapeDtypeStruct((rows, width), jnp.bfloat16),
            jax.ShapeDtypeStruct((rows, 2 * kv_width), jnp.bfloat16),
        ),
        in_specs=[scalars] * 3 + [anywhere] * 3,
        out_specs=(anywhere, anywhere, anywhere),
        scratch_shapes=[
            wide, narrow, wide, wide, wide, narrow,
            ring, pltpu.VMEM((groups, 2, rows, HEAD), jnp.float32), ring, ring,
            dma((groups, 2)), dma, dma((groups, 2)), dma,
            dma((groups, 4, 2)), dma((groups, 4, 2)), dma((groups, 4)), dma((groups, 4)),
        ],
        compiler_params=pltpu.CompilerParams(
            collective_id=0, has_side_effects=True, vmem_limit_bytes=40 * 1024 * 1024
        ),
    )(key_blocks, key_count, block_at_slot, queries, keys_values, out_grad)


def solution(mesh):
    sharded = P(("groups", "ctx"), None)
    return jax.shard_map(
        body,
        mesh=mesh,
        in_specs=(sharded, sharded, sharded, P("groups", None), P("groups"), P("groups")),
        out_specs=(sharded, sharded, sharded),
        check_vma=False,
    )
```

```python
import functools

import jax
import jax.numpy as jnp
from jax import lax
from jax.experimental import pallas as pl
from jax.experimental.pallas import tpu as pltpu
from jax.sharding import PartitionSpec as P

HEAD = 128
OFFSETS = (-2, -1, 1, 2)
LOG2E = 1.4426950408889634
NEG = -1e30
NT = (((1,), (1,)), ((), ()))


def kernel(
    n, groups, repeats,
    blocks_ref, count_ref, slot_ref, q_hbm, kv_hbm, do_hbm,
    att_hbm, dq_hbm, kvg_hbm,
    q, kv, do, att, dq, kvg, near, own_grad, gsend, grecv,
    in_sem, kv_sem, out_sem, kvg_sem, near_send, near_recv, grad_send, grad_recv,
):
    rows = q.shape[0]
    wide = repeats * HEAD
    kv_width = groups * HEAD
    scale = HEAD ** (-0.5)
    me = lax.axis_index("ctx")

    def exists(o):
        return jnp.logical_and(me + OFFSETS[o] >= 0, me + OFFSETS[o] < n)

    def exists_at(slot):
        there = me + jnp.where(slot < 2, slot - 2, slot - 1)
        return jnp.logical_and(there >= 0, there < n)

    def target(o):
        return {"ctx": me + OFFSETS[o]}

    def column(g, width):
        return pl.ds(pl.multiple_of(g * width, width), width)

    core = lax.rem(me, 2)
    sibling = {"ctx": me + 1 - 2 * core}
    forward = 3 * (1 - core)
    passed = 1 + core
    beside = 2 - core

    def own_part(g, part):
        return kv.at[:, pl.ds(pl.multiple_of(part * kv_width + g * HEAD, HEAD), HEAD)]

    def remote(src, dst, sent, received, device):
        return pltpu.make_async_remote_copy(
            src_ref=src, dst_ref=dst, send_sem=sent, recv_sem=received,
            device_id=device, device_id_type=pl.DeviceIdType.MESH,
        )

    def far_copy(g, o, part):
        return remote(
            own_part(g, part), near.at[g, 3 - o, part],
            near_send.at[g, o, part], near_recv.at[g, 3 - o, part], target(o),
        )

    def beside_copy(g, part):
        return remote(
            own_part(g, part), near.at[g, 1 + core, part],
            near_send.at[g, 1, part], near_recv.at[g, 1 + core, part], sibling,
        )

    def relay_copy(g, part):
        return remote(
            near.at[g, forward, part], near.at[g, 2 - core, part],
            near_send.at[g, 2, part], near_recv.at[g, 2 - core, part], sibling,
        )

    def near_wait(g, slot):
        for part in range(2):
            remote(
                near.at[g, slot, part], near.at[g, slot, part],
                near_send.at[g, 0, part], near_recv.at[g, slot, part], sibling,
            ).wait_recv()

    def far_grad(g, o):
        return remote(
            gsend.at[g, o], grecv.at[g, 3 - o], grad_send.at[g, o], grad_recv.at[g, 3 - o], target(o)
        )

    def beside_grad(g):
        return remote(gsend.at[g, beside], grecv.at[g, 1], grad_send.at[g, 1], grad_recv.at[g, 1], sibling)

    def passed_grad(g):
        return remote(gsend.at[g, passed], grecv.at[g, 2], grad_send.at[g, 2], grad_recv.at[g, 2], sibling)

    def relay(g):
        @pl.when(exists_at(forward))
        def _():
            near_wait(g, forward)
            relay_copy(g, 0).start()
            relay_copy(g, 1).start()

    def combine(g):
        @pl.when(exists_at(forward))
        def _():
            passed_grad(g).wait_recv()
            both = gsend[g, forward].astype(jnp.float32) + grecv[g, 2].astype(jnp.float32)
            gsend[g, forward] = both.astype(jnp.bfloat16)

        for o, mine in ((3, 0), (0, 1)):

            @pl.when(jnp.logical_and(exists(o), core == mine))
            def _():
                far_grad(g, o).start()

    def load_copies(g):
        return (
            pltpu.make_async_copy(q_hbm.at[:, column(g, wide)], q.at[:, column(g, wide)], in_sem.at[g, 0]),
            pltpu.make_async_copy(do_hbm.at[:, column(g, wide)], do.at[:, column(g, wide)], in_sem.at[g, 1]),
        )

    def store_copies(g):
        return (
            pltpu.make_async_copy(att.at[:, column(g, wide)], att_hbm.at[:, column(g, wide)], out_sem.at[g, 0]),
            pltpu.make_async_copy(dq.at[:, column(g, wide)], dq_hbm.at[:, column(g, wide)], out_sem.at[g, 1]),
        )

    kv_load = pltpu.make_async_copy(kv_hbm, kv, kv_sem)

    kv_load.start()
    for copy in load_copies(0):
        copy.start()
    barrier = pltpu.get_barrier_semaphore()
    pl.semaphore_signal(barrier, inc=1, device_id=sibling, device_id_type=pl.DeviceIdType.MESH)
    for o in (0, 3):

        @pl.when(exists(o))
        def _():
            pl.semaphore_signal(barrier, inc=1, device_id=target(o), device_id_type=pl.DeviceIdType.MESH)

    for o in range(4):

        @pl.when(jnp.logical_not(exists(o)))
        def _():
            near[:, o] = jnp.zeros((groups, 2, rows, HEAD), near.dtype)
            if o in (0, 3):
                grecv[:, o] = jnp.zeros((groups, 2, rows, HEAD), grecv.dtype)

    kv_load.wait()
    pl.semaphore_wait(barrier, 1 + exists(0).astype(jnp.int32) + exists(3).astype(jnp.int32))

    for g in range(groups):
        for o in (3, 0):

            @pl.when(exists(o))
            def _():
                far_copy(g, o, 0).start()
                far_copy(g, o, 1).start()

        beside_copy(g, 0).start()
        beside_copy(g, 1).start()
        if g > 0:
            for copy in load_copies(g):
                copy.start()

    own_block = slot_ref[me]
    live_count = count_ref[own_block]
    chosen = []
    bias = []
    for j in (1, 2):
        wanted = blocks_ref[j, own_block]
        hits = []
        for o in range(4):
            there = jnp.clip(me + OFFSETS[o], 0, n - 1)
            hits.append(exists(o) & (slot_ref[there] == wanted) & (live_count > j))
        chosen.append(hits)
        bias.append(jnp.where(hits[0] | hits[1] | hits[2] | hits[3], 0.0, NEG).astype(jnp.float32))

    def pick(g, part, hits):
        value = near[g, 0, part]
        for o in range(1, 4):
            value = jnp.where(hits[o], near[g, o, part], value)
        return value

    def step(g, carry):
        for copy in load_copies(g):
            copy.wait()
        near_wait(g, beside)

        @pl.when(exists_at(3 - forward))
        def _():
            near_wait(g, 3 - forward)

        @pl.when(exists_at(passed))
        def _():
            near_wait(g, passed)

        @pl.when(g > 0)
        def _():
            combine(g - 1)

        own_key = kv[:, pl.ds(pl.multiple_of(g * HEAD, HEAD), HEAD)]
        own_value = kv[:, pl.ds(pl.multiple_of(kv_width + g * HEAD, HEAD), HEAD)]
        keys = jnp.concatenate([own_key, pick(g, 0, chosen[0]), pick(g, 0, chosen[1])], axis=0)
        values = jnp.concatenate([own_value, pick(g, 1, chosen[0]), pick(g, 1, chosen[1])], axis=0)
        keys_t = keys.T
        values_t = values.T
        key_grad = jnp.zeros((3 * rows, HEAD), jnp.float32)
        value_grad = jnp.zeros((3 * rows, HEAD), jnp.float32)
        for pair in range(repeats // 2):
            starts = [pl.multiple_of(g * wide + (2 * pair + i) * HEAD, HEAD) for i in range(2)]
            q2 = jnp.concatenate([q[:, pl.ds(s, HEAD)] for s in starts], axis=0)
            do2 = jnp.concatenate([do[:, pl.ds(s, HEAD)] for s in starts], axis=0)
            raw = lax.dot_general(keys, q2, NT, preferred_element_type=jnp.float32) * (scale * LOG2E)
            scores = jnp.concatenate(
                [raw[:rows], raw[rows : 2 * rows] + bias[0], raw[2 * rows :] + bias[1]], axis=0
            )
            best = jnp.max(scores, axis=0, keepdims=True)
            weights = jnp.exp2(scores - best)
            total = jnp.sum(weights, axis=0, keepdims=True)
            probs = weights * (1.0 / total)
            rounded = probs.astype(jnp.bfloat16)
            prob_grads = lax.dot_general(values, do2, NT, preferred_element_type=jnp.float32)
            delta = jnp.sum(probs * prob_grads, axis=0, keepdims=True)
            score_grads = (probs * (prob_grads - delta)).astype(jnp.bfloat16)
            mixed = jnp.dot(values_t, rounded, preferred_element_type=jnp.float32)
            query_grad = jnp.dot(keys_t, score_grads, preferred_element_type=jnp.float32) * scale
            mixed = mixed.astype(jnp.bfloat16).T
            query_grad = query_grad.astype(jnp.bfloat16).T
            for i in range(2):
                att[:, pl.ds(starts[i], HEAD)] = mixed[i * rows : (i + 1) * rows]
                dq[:, pl.ds(starts[i], HEAD)] = query_grad[i * rows : (i + 1) * rows]
            if pair == 1:

                @pl.when(g + 1 < groups)
                def _():
                    relay(g + 1)

            key_grad = key_grad + jnp.dot(score_grads, q2, preferred_element_type=jnp.float32)
            value_grad = value_grad + jnp.dot(rounded, do2, preferred_element_type=jnp.float32)
        for part, grad in ((0, key_grad * scale), (1, value_grad)):
            own_grad[g, part] = grad[:rows]
            for o in range(4):
                gsend[g, o, part] = jnp.where(
                    chosen[0][o], grad[rows : 2 * rows], jnp.where(chosen[1][o], grad[2 * rows :], 0.0)
                ).astype(jnp.bfloat16)
        @pl.when(exists_at(passed))
        def _():
            passed_grad(g).start()

        for o, mine in ((3, 1), (0, 0)):

            @pl.when(jnp.logical_and(exists(o), core == mine))
            def _():
                far_grad(g, o).start()

        beside_grad(g).start()
        for copy in store_copies(g):
            copy.start()
        return carry

    relay(0)
    lax.fori_loop(0, groups, step, 0)
    combine(groups - 1)

    def finish(g, carry):
        for o in (0, 3):

            @pl.when(exists(3 - o))
            def _():
                far_grad(g, o).wait_recv()

        beside_grad(g).wait_recv()

        for part in range(2):
            total = own_grad[g, part]
            for o in (0, 1, 3):
                total = total + grecv[g, o, part].astype(jnp.float32)
            kvg[:, pl.ds(pl.multiple_of(part * kv_width + g * HEAD, HEAD), HEAD)] = total.astype(jnp.bfloat16)
        return carry

    lax.fori_loop(0, groups, finish, 0)
    kvg_store = pltpu.make_async_copy(kvg, kvg_hbm, kvg_sem)
    kvg_store.start()

    def drain(g, carry):
        for o in (0, 3):

            @pl.when(exists(o))
            def _():
                far_copy(g, o, 0).wait_send()
                far_copy(g, o, 1).wait_send()
                far_grad(g, o).wait_send()

        @pl.when(exists_at(forward))
        def _():
            relay_copy(g, 0).wait_send()
            relay_copy(g, 1).wait_send()

        @pl.when(exists_at(passed))
        def _():
            passed_grad(g).wait_send()

        beside_copy(g, 0).wait_send()
        beside_copy(g, 1).wait_send()
        beside_grad(g).wait_send()
        for copy in store_copies(g):
            copy.wait()
        return carry

    lax.fori_loop(0, groups, drain, 0)
    kvg_store.wait()


def body(queries, keys_values, out_grad, key_blocks, key_count, block_at_slot):
    n = lax.axis_size("ctx")
    rows, width = queries.shape
    kv_width = keys_values.shape[1] // 2
    groups = kv_width // HEAD
    repeats = width // kv_width
    anywhere = pl.BlockSpec(memory_space=pl.ANY)
    scalars = pl.BlockSpec(memory_space=pltpu.SMEM)
    wide = pltpu.VMEM((rows, width), jnp.bfloat16)
    narrow = pltpu.VMEM((rows, 2 * kv_width), jnp.bfloat16)
    ring = pltpu.VMEM((groups, 4, 2, rows, HEAD), jnp.bfloat16)
    dma = pltpu.SemaphoreType.DMA
    return pl.pallas_call(
        functools.partial(kernel, n, groups, repeats),
        out_shape=(
            jax.ShapeDtypeStruct((rows, width), jnp.bfloat16),
            jax.ShapeDtypeStruct((rows, width), jnp.bfloat16),
            jax.ShapeDtypeStruct((rows, 2 * kv_width), jnp.bfloat16),
        ),
        in_specs=[scalars] * 3 + [pl.BlockSpec(memory_space=pltpu.HBM)] * 3,
        out_specs=(anywhere, anywhere, anywhere),
        scratch_shapes=[
            wide, narrow, wide, wide, wide, narrow,
            ring, pltpu.VMEM((groups, 2, rows, HEAD), jnp.float32), ring, ring,
            dma((groups, 2)), dma, dma((groups, 2)), dma,
            dma((groups, 4, 2)), dma((groups, 4, 2)), dma((groups, 4)), dma((groups, 4)),
        ],
        compiler_params=pltpu.CompilerParams(
            collective_id=0, has_side_effects=True, vmem_limit_bytes=40 * 1024 * 1024
        ),
    )(key_blocks.T, key_count, block_at_slot, queries, keys_values, out_grad)


def solution(mesh):
    sharded = P(("groups", "ctx"), None)
    return jax.shard_map(
        body,
        mesh=mesh,
        in_specs=(sharded, sharded, sharded, P("groups", None), P("groups"), P("groups")),
        out_specs=(sharded, sharded, sharded),
        check_vma=False,
    )
```

```python
import functools

import jax
import jax.numpy as jnp
from jax import lax
from jax.experimental import pallas as pl
from jax.experimental.pallas import tpu as pltpu
from jax.sharding import PartitionSpec as P

HEAD = 128
OFFSETS = (-2, -1, 1, 2)
LOG2E = 1.4426950408889634
NEG = -1e30
NT = (((1,), (1,)), ((), ()))


def kernel(
    n, groups, repeats,
    blocks_ref, count_ref, slot_ref, q_hbm, kv_hbm, do_hbm,
    att_hbm, dq_hbm, kvg_hbm,
    q, kv, do, att, dq, kvg, near, own_grad, gsend, grecv,
    in_sem, kv_sem, out_sem, kvg_sem, near_send, near_recv, grad_send, grad_recv,
):
    rows = q.shape[0]
    wide = repeats * HEAD
    kv_width = groups * HEAD
    scale = HEAD ** (-0.5)
    me = lax.axis_index("ctx")

    def exists(o):
        return jnp.logical_and(me + OFFSETS[o] >= 0, me + OFFSETS[o] < n)

    def exists_at(slot):
        there = me + jnp.where(slot < 2, slot - 2, slot - 1)
        return jnp.logical_and(there >= 0, there < n)

    def target(o):
        return {"ctx": me + OFFSETS[o]}

    def column(g, width):
        return pl.ds(pl.multiple_of(g * width, width), width)

    core = lax.rem(me, 2)
    sibling = {"ctx": me + 1 - 2 * core}
    forward = 3 * (1 - core)
    passed = 1 + core
    beside = 2 - core

    def remote(src, dst, sent, received, device):
        return pltpu.make_async_remote_copy(
            src_ref=src, dst_ref=dst, send_sem=sent, recv_sem=received,
            device_id=device, device_id_type=pl.DeviceIdType.MESH,
        )

    def far_copy(g, o):
        return remote(kv.at[g], near.at[g, 3 - o], near_send.at[g, o], near_recv.at[g, 3 - o], target(o))

    def beside_copy(g):
        return remote(
            kv.at[g], near.at[g, 1 + core], near_send.at[g, 1], near_recv.at[g, 1 + core], sibling
        )

    def relay_copy(g):
        return remote(
            near.at[g, forward], near.at[g, 2 - core], near_send.at[g, 2], near_recv.at[g, 2 - core], sibling
        )

    def near_wait(g, slot):
        remote(
            near.at[g, slot], near.at[g, slot], near_send.at[g, 0], near_recv.at[g, slot], sibling
        ).wait_recv()

    def kv_load(g, part):
        return pltpu.make_async_copy(
            kv_hbm.at[:, pl.ds(part * kv_width + g * HEAD, HEAD)], kv.at[g, part], kv_sem.at[g, part]
        )

    def far_grad(g, o):
        return remote(
            gsend.at[g, o], grecv.at[g, 3 - o], grad_send.at[g, o], grad_recv.at[g, 3 - o], target(o)
        )

    def beside_grad(g):
        return remote(gsend.at[g, beside], grecv.at[g, 1], grad_send.at[g, 1], grad_recv.at[g, 1], sibling)

    def passed_grad(g):
        return remote(gsend.at[g, passed], grecv.at[g, 2], grad_send.at[g, 2], grad_recv.at[g, 2], sibling)

    def relay(g):
        @pl.when(exists_at(forward))
        def _():
            near_wait(g, forward)
            relay_copy(g).start()

    def combine(g):
        @pl.when(exists_at(forward))
        def _():
            passed_grad(g).wait_recv()
            both = gsend[g, forward].astype(jnp.float32) + grecv[g, 2].astype(jnp.float32)
            gsend[g, forward] = both.astype(jnp.bfloat16)

        for o, mine in ((3, 0), (0, 1)):

            @pl.when(jnp.logical_and(exists(o), core == mine))
            def _():
                far_grad(g, o).start()

    def load_copies(g):
        return (
            pltpu.make_async_copy(q_hbm.at[:, column(g, wide)], q.at[:, column(g, wide)], in_sem.at[g, 0]),
            pltpu.make_async_copy(do_hbm.at[:, column(g, wide)], do.at[:, column(g, wide)], in_sem.at[g, 1]),
        )

    def store_copies(g):
        return (
            pltpu.make_async_copy(att.at[:, column(g, wide)], att_hbm.at[:, column(g, wide)], out_sem.at[g, 0]),
            pltpu.make_async_copy(dq.at[:, column(g, wide)], dq_hbm.at[:, column(g, wide)], out_sem.at[g, 1]),
        )

    for g in range(groups):
        for part in range(2):
            kv_load(g, part).start()
    for copy in load_copies(0):
        copy.start()
    barrier = pltpu.get_barrier_semaphore()
    pl.semaphore_signal(barrier, inc=1, device_id=sibling, device_id_type=pl.DeviceIdType.MESH)
    for o in (0, 3):

        @pl.when(exists(o))
        def _():
            pl.semaphore_signal(barrier, inc=1, device_id=target(o), device_id_type=pl.DeviceIdType.MESH)

    for o in range(4):

        @pl.when(jnp.logical_not(exists(o)))
        def _():
            near[:, o] = jnp.zeros((groups, 2, rows, HEAD), near.dtype)
            if o in (0, 3):
                grecv[:, o] = jnp.zeros((groups, 2, rows, HEAD), grecv.dtype)

    pl.semaphore_wait(barrier, 1 + exists(0).astype(jnp.int32) + exists(3).astype(jnp.int32))

    for g in range(groups):
        kv_load(g, 0).wait()
        kv_load(g, 1).wait()
        for o in (3, 0):

            @pl.when(exists(o))
            def _():
                far_copy(g, o).start()

        beside_copy(g).start()
        if g > 0:
            for copy in load_copies(g):
                copy.start()

    own_block = slot_ref[me]
    live_count = count_ref[own_block]
    chosen = []
    bias = []
    for j in (1, 2):
        wanted = blocks_ref[j, own_block]
        hits = []
        for o in range(4):
            there = jnp.clip(me + OFFSETS[o], 0, n - 1)
            hits.append(exists(o) & (slot_ref[there] == wanted) & (live_count > j))
        chosen.append(hits)
        bias.append(jnp.where(hits[0] | hits[1] | hits[2] | hits[3], 0.0, NEG).astype(jnp.float32))

    def pick(g, part, hits):
        value = near[g, 0, part]
        for o in range(1, 4):
            value = jnp.where(hits[o], near[g, o, part], value)
        return value

    def step(g, carry):
        for copy in load_copies(g):
            copy.wait()
        near_wait(g, beside)

        @pl.when(exists_at(3 - forward))
        def _():
            near_wait(g, 3 - forward)

        @pl.when(exists_at(passed))
        def _():
            near_wait(g, passed)

        @pl.when(g > 0)
        def _():
            combine(g - 1)

        own_key = kv[g, 0]
        own_value = kv[g, 1]
        keys = jnp.concatenate([own_key, pick(g, 0, chosen[0]), pick(g, 0, chosen[1])], axis=0)
        values = jnp.concatenate([own_value, pick(g, 1, chosen[0]), pick(g, 1, chosen[1])], axis=0)
        keys_t = keys.T
        values_t = values.T
        key_grad = jnp.zeros((3 * rows, HEAD), jnp.float32)
        value_grad = jnp.zeros((3 * rows, HEAD), jnp.float32)
        for pair in range(repeats // 2):
            starts = [pl.multiple_of(g * wide + (2 * pair + i) * HEAD, HEAD) for i in range(2)]
            q2 = jnp.concatenate([q[:, pl.ds(s, HEAD)] for s in starts], axis=0)
            do2 = jnp.concatenate([do[:, pl.ds(s, HEAD)] for s in starts], axis=0)
            raw = lax.dot_general(keys, q2, NT, preferred_element_type=jnp.float32) * (scale * LOG2E)
            scores = jnp.concatenate(
                [raw[:rows], raw[rows : 2 * rows] + bias[0], raw[2 * rows :] + bias[1]], axis=0
            )
            best = jnp.max(scores, axis=0, keepdims=True)
            weights = jnp.exp2(scores - best)
            total = jnp.sum(weights, axis=0, keepdims=True)
            probs = weights * (1.0 / total)
            rounded = probs.astype(jnp.bfloat16)
            prob_grads = lax.dot_general(values, do2, NT, preferred_element_type=jnp.float32)
            delta = jnp.sum(probs * prob_grads, axis=0, keepdims=True)
            score_grads = (probs * (prob_grads - delta)).astype(jnp.bfloat16)
            mixed = jnp.dot(values_t, rounded, preferred_element_type=jnp.float32)
            query_grad = jnp.dot(keys_t, score_grads, preferred_element_type=jnp.float32) * scale
            mixed = mixed.astype(jnp.bfloat16).T
            query_grad = query_grad.astype(jnp.bfloat16).T
            for i in range(2):
                att[:, pl.ds(starts[i], HEAD)] = mixed[i * rows : (i + 1) * rows]
                dq[:, pl.ds(starts[i], HEAD)] = query_grad[i * rows : (i + 1) * rows]
            if pair == 1:

                @pl.when(g + 1 < groups)
                def _():
                    relay(g + 1)

            key_grad = key_grad + jnp.dot(score_grads, q2, preferred_element_type=jnp.float32)
            value_grad = value_grad + jnp.dot(rounded, do2, preferred_element_type=jnp.float32)
        for part, grad in ((0, key_grad * scale), (1, value_grad)):
            own_grad[g, part] = grad[:rows]
            for o in range(4):
                gsend[g, o, part] = jnp.where(
                    chosen[0][o], grad[rows : 2 * rows], jnp.where(chosen[1][o], grad[2 * rows :], 0.0)
                ).astype(jnp.bfloat16)
        @pl.when(exists_at(passed))
        def _():
            passed_grad(g).start()

        for o, mine in ((3, 1), (0, 0)):

            @pl.when(jnp.logical_and(exists(o), core == mine))
            def _():
                far_grad(g, o).start()

        beside_grad(g).start()
        for copy in store_copies(g):
            copy.start()
        return carry

    relay(0)
    lax.fori_loop(0, groups, step, 0)
    combine(groups - 1)

    def finish(g, carry):
        for o in (0, 3):

            @pl.when(exists(3 - o))
            def _():
                far_grad(g, o).wait_recv()

        beside_grad(g).wait_recv()

        for part in range(2):
            total = own_grad[g, part]
            for o in (0, 1, 3):
                total = total + grecv[g, o, part].astype(jnp.float32)
            kvg[:, pl.ds(pl.multiple_of(part * kv_width + g * HEAD, HEAD), HEAD)] = total.astype(jnp.bfloat16)
        return carry

    lax.fori_loop(0, groups, finish, 0)
    kvg_store = pltpu.make_async_copy(kvg, kvg_hbm, kvg_sem)
    kvg_store.start()

    def drain(g, carry):
        for o in (0, 3):

            @pl.when(exists(o))
            def _():
                far_copy(g, o).wait_send()
                far_grad(g, o).wait_send()

        @pl.when(exists_at(forward))
        def _():
            relay_copy(g).wait_send()

        @pl.when(exists_at(passed))
        def _():
            passed_grad(g).wait_send()

        beside_copy(g).wait_send()
        beside_grad(g).wait_send()
        for copy in store_copies(g):
            copy.wait()
        return carry

    lax.fori_loop(0, groups, drain, 0)
    kvg_store.wait()


def flush(att, dq, kvg, att_out, dq_out, kvg_out, sem):
    copies = [
        pltpu.make_async_copy(source, result, sem.at[i])
        for i, (source, result) in enumerate(((att, att_out), (dq, dq_out), (kvg, kvg_out)))
    ]
    for copy in copies:
        copy.start()
    for copy in copies:
        copy.wait()


def body(queries, keys_values, out_grad, key_blocks, key_count, block_at_slot):
    n = lax.axis_size("ctx")
    rows, width = queries.shape
    kv_width = keys_values.shape[1] // 2
    groups = kv_width // HEAD
    repeats = width // kv_width
    anywhere = pl.BlockSpec(memory_space=pl.ANY)
    scalars = pl.BlockSpec(memory_space=pltpu.SMEM)
    wide = pltpu.VMEM((rows, width), jnp.bfloat16)
    narrow = pltpu.VMEM((rows, 2 * kv_width), jnp.bfloat16)
    ring = pltpu.VMEM((groups, 4, 2, rows, HEAD), jnp.bfloat16)
    dma = pltpu.SemaphoreType.DMA
    shapes = (
        jax.ShapeDtypeStruct((rows, width), jnp.bfloat16),
        jax.ShapeDtypeStruct((rows, width), jnp.bfloat16),
        jax.ShapeDtypeStruct((rows, 2 * kv_width), jnp.bfloat16),
    )
    results = pl.pallas_call(
        functools.partial(kernel, n, groups, repeats),
        out_shape=shapes,
        in_specs=[scalars] * 3 + [pl.BlockSpec(memory_space=pltpu.HBM)] * 3,
        out_specs=(anywhere, anywhere, anywhere),
        scratch_shapes=[
            wide, pltpu.VMEM((groups, 2, rows, HEAD), jnp.bfloat16), wide, wide, wide, narrow,
            ring, pltpu.VMEM((groups, 2, rows, HEAD), jnp.float32), ring, ring,
            dma((groups, 2)), dma((groups, 2)), dma((groups, 2)), dma,
            dma((groups, 4)), dma((groups, 4)), dma((groups, 4)), dma((groups, 4)),
        ],
        compiler_params=pltpu.CompilerParams(
            collective_id=0, has_side_effects=True, vmem_limit_bytes=40 * 1024 * 1024
        ),
    )(key_blocks.T, key_count, block_at_slot, queries, keys_values, out_grad)
    return pl.pallas_call(
        flush,
        out_shape=shapes,
        in_specs=[anywhere] * 3,
        out_specs=(pl.BlockSpec(memory_space=pltpu.HBM),) * 3,
        scratch_shapes=[dma((3,))],
        compiler_params=pltpu.CompilerParams(vmem_limit_bytes=1024 * 1024),
    )(*results)


def solution(mesh):
    sharded = P(("groups", "ctx"), None)
    return jax.shard_map(
        body,
        mesh=mesh,
        in_specs=(sharded, sharded, sharded, P("groups", None), P("groups"), P("groups")),
        out_specs=(sharded, sharded, sharded),
        check_vma=False,
    )
```

```python
import functools

import jax
import jax.numpy as jnp
from jax import lax
from jax.experimental import pallas as pl
from jax.experimental.pallas import tpu as pltpu
from jax.sharding import PartitionSpec as P

HEAD = 128
OFFSETS = (-2, -1, 1, 2)
LOG2E = 1.4426950408889634
NEG = -1e30
NT = (((1,), (1,)), ((), ()))


def kernel(
    n, groups, repeats,
    blocks_ref, count_ref, slot_ref, q_hbm, kv_hbm, do_hbm,
    att_hbm, dq_hbm, kvg_hbm,
    q, kv, do, att, dq, kvg, near, own_grad, gsend, grecv,
    in_sem, kv_sem, out_sem, kvg_sem, near_send, near_recv, grad_send, grad_recv,
):
    rows = q.shape[0]
    wide = repeats * HEAD
    kv_width = groups * HEAD
    scale = HEAD ** (-0.5)
    me = lax.axis_index("ctx")

    def exists(o):
        return jnp.logical_and(me + OFFSETS[o] >= 0, me + OFFSETS[o] < n)

    def exists_at(slot):
        there = me + jnp.where(slot < 2, slot - 2, slot - 1)
        return jnp.logical_and(there >= 0, there < n)

    def target(o):
        return {"ctx": me + OFFSETS[o]}

    def column(g, width):
        return pl.ds(pl.multiple_of(g * width, width), width)

    core = lax.rem(me, 2)
    sibling = {"ctx": me + 1 - 2 * core}
    forward = 3 * (1 - core)
    passed = 1 + core
    beside = 2 - core

    def remote(src, dst, sent, received, device):
        return pltpu.make_async_remote_copy(
            src_ref=src, dst_ref=dst, send_sem=sent, recv_sem=received,
            device_id=device, device_id_type=pl.DeviceIdType.MESH,
        )

    def far_copy(g, o):
        return remote(kv.at[g], near.at[g, 3 - o], near_send.at[g, o], near_recv.at[g, 3 - o], target(o))

    def beside_copy(g):
        return remote(
            kv.at[g], near.at[g, 1 + core], near_send.at[g, 1], near_recv.at[g, 1 + core], sibling
        )

    def relay_copy(g):
        return remote(
            near.at[g, forward], near.at[g, 2 - core], near_send.at[g, 2], near_recv.at[g, 2 - core], sibling
        )

    def near_wait(g, slot):
        remote(
            near.at[g, slot], near.at[g, slot], near_send.at[g, 0], near_recv.at[g, slot], sibling
        ).wait_recv()

    def kv_load(g, part):
        return pltpu.make_async_copy(
            kv_hbm.at[:, pl.ds(part * kv_width + g * HEAD, HEAD)], kv.at[g, part], kv_sem.at[g, part]
        )

    def far_grad(g, o):
        return remote(
            gsend.at[g, o], grecv.at[g, 3 - o], grad_send.at[g, o], grad_recv.at[g, 3 - o], target(o)
        )

    def beside_grad(g):
        return remote(gsend.at[g, beside], grecv.at[g, 1], grad_send.at[g, 1], grad_recv.at[g, 1], sibling)

    def passed_grad(g):
        return remote(gsend.at[g, passed], grecv.at[g, 2], grad_send.at[g, 2], grad_recv.at[g, 2], sibling)

    def relay(g):
        @pl.when(exists_at(forward))
        def _():
            near_wait(g, forward)
            relay_copy(g).start()

    def combine(g):
        @pl.when(exists_at(forward))
        def _():
            passed_grad(g).wait_recv()
            both = gsend[g, forward].astype(jnp.float32) + grecv[g, 2].astype(jnp.float32)
            gsend[g, forward] = both.astype(jnp.bfloat16)

        for o, mine in ((3, 0), (0, 1)):

            @pl.when(jnp.logical_and(exists(o), core == mine))
            def _():
                far_grad(g, o).start()

    def load_copies(g):
        return (
            pltpu.make_async_copy(q_hbm.at[:, column(g, wide)], q.at[:, column(g, wide)], in_sem.at[g, 0]),
            pltpu.make_async_copy(do_hbm.at[:, column(g, wide)], do.at[:, column(g, wide)], in_sem.at[g, 1]),
        )

    def store_copies(g):
        return (
            pltpu.make_async_copy(att.at[:, column(g, wide)], att_hbm.at[:, column(g, wide)], out_sem.at[g, 0]),
            pltpu.make_async_copy(dq.at[:, column(g, wide)], dq_hbm.at[:, column(g, wide)], out_sem.at[g, 1]),
        )

    for g in range(groups):
        for part in range(2):
            kv_load(g, part).start()
    for copy in load_copies(0):
        copy.start()
    barrier = pltpu.get_barrier_semaphore()
    pl.semaphore_signal(barrier, inc=1, device_id=sibling, device_id_type=pl.DeviceIdType.MESH)
    for o in (0, 3):

        @pl.when(exists(o))
        def _():
            pl.semaphore_signal(barrier, inc=1, device_id=target(o), device_id_type=pl.DeviceIdType.MESH)

    for o in range(4):

        @pl.when(jnp.logical_not(exists(o)))
        def _():
            near[:, o] = jnp.zeros((groups, 2, rows, HEAD), near.dtype)
            if o in (0, 3):
                grecv[:, o] = jnp.zeros((groups, 2, rows, HEAD), grecv.dtype)

    pl.semaphore_wait(barrier, 1 + exists(0).astype(jnp.int32) + exists(3).astype(jnp.int32))

    for g in range(groups):
        kv_load(g, 0).wait()
        kv_load(g, 1).wait()
        for o in (3, 0):

            @pl.when(exists(o))
            def _():
                far_copy(g, o).start()

        beside_copy(g).start()
        if g > 0:
            for copy in load_copies(g):
                copy.start()

    own_block = slot_ref[me]
    live_count = count_ref[own_block]
    chosen = []
    bias = []
    for j in (1, 2):
        wanted = blocks_ref[j, own_block]
        hits = []
        for o in range(4):
            there = jnp.clip(me + OFFSETS[o], 0, n - 1)
            hits.append(exists(o) & (slot_ref[there] == wanted) & (live_count > j))
        chosen.append(hits)
        bias.append(jnp.where(hits[0] | hits[1] | hits[2] | hits[3], 0.0, NEG).astype(jnp.float32))

    def pick(g, part, hits):
        value = near[g, 0, part]
        for o in range(1, 4):
            value = jnp.where(hits[o], near[g, o, part], value)
        return value

    def step(g, carry):
        for copy in load_copies(g):
            copy.wait()
        near_wait(g, beside)

        @pl.when(exists_at(3 - forward))
        def _():
            near_wait(g, 3 - forward)

        @pl.when(exists_at(passed))
        def _():
            near_wait(g, passed)

        @pl.when(g > 0)
        def _():
            combine(g - 1)

        own_key = kv[g, 0]
        own_value = kv[g, 1]
        keys = jnp.concatenate([own_key, pick(g, 0, chosen[0]), pick(g, 0, chosen[1])], axis=0)
        values = jnp.concatenate([own_value, pick(g, 1, chosen[0]), pick(g, 1, chosen[1])], axis=0)
        keys_t = keys.T
        values_t = values.T
        key_grad = jnp.zeros((3 * rows, HEAD), jnp.float32)
        value_grad = jnp.zeros((3 * rows, HEAD), jnp.float32)
        for pair in range(repeats // 2):
            starts = [pl.multiple_of(g * wide + (2 * pair + i) * HEAD, HEAD) for i in range(2)]
            q2 = jnp.concatenate([q[:, pl.ds(s, HEAD)] for s in starts], axis=0)
            do2 = jnp.concatenate([do[:, pl.ds(s, HEAD)] for s in starts], axis=0)
            raw = lax.dot_general(keys, q2, NT, preferred_element_type=jnp.float32) * (scale * LOG2E)
            scores = jnp.concatenate(
                [raw[:rows], raw[rows : 2 * rows] + bias[0], raw[2 * rows :] + bias[1]], axis=0
            )
            best = jnp.max(scores, axis=0, keepdims=True)
            weights = jnp.exp2(scores - best)
            total = jnp.sum(weights, axis=0, keepdims=True)
            probs = weights * (1.0 / total)
            rounded = probs.astype(jnp.bfloat16)
            prob_grads = lax.dot_general(values, do2, NT, preferred_element_type=jnp.float32)
            delta = jnp.sum(probs * prob_grads, axis=0, keepdims=True)
            score_grads = (probs * (prob_grads - delta)).astype(jnp.bfloat16)
            mixed = jnp.dot(values_t, rounded, preferred_element_type=jnp.float32)
            query_grad = jnp.dot(keys_t, score_grads, preferred_element_type=jnp.float32) * scale
            mixed = mixed.astype(jnp.bfloat16).T
            query_grad = query_grad.astype(jnp.bfloat16).T
            for i in range(2):
                att[:, pl.ds(starts[i], HEAD)] = mixed[i * rows : (i + 1) * rows]
                dq[:, pl.ds(starts[i], HEAD)] = query_grad[i * rows : (i + 1) * rows]
            if pair == 1:

                @pl.when(g + 1 < groups)
                def _():
                    relay(g + 1)

            key_grad = key_grad + jnp.dot(score_grads, q2, preferred_element_type=jnp.float32)
            value_grad = value_grad + jnp.dot(rounded, do2, preferred_element_type=jnp.float32)
        for part, grad in ((0, key_grad * scale), (1, value_grad)):
            own_grad[g, part] = grad[:rows]
            for o in range(4):
                gsend[g, o, part] = jnp.where(
                    chosen[0][o], grad[rows : 2 * rows], jnp.where(chosen[1][o], grad[2 * rows :], 0.0)
                ).astype(jnp.bfloat16)
        @pl.when(exists_at(passed))
        def _():
            passed_grad(g).start()

        for o, mine in ((3, 1), (0, 0)):

            @pl.when(jnp.logical_and(exists(o), core == mine))
            def _():
                far_grad(g, o).start()

        beside_grad(g).start()
        for copy in store_copies(g):
            copy.start()
        return carry

    relay(0)
    lax.fori_loop(0, groups, step, 0)
    combine(groups - 1)

    def finish(g, carry):
        for o in (0, 3):

            @pl.when(exists(3 - o))
            def _():
                far_grad(g, o).wait_recv()

        beside_grad(g).wait_recv()

        for part in range(2):
            total = own_grad[g, part]
            for o in (0, 1, 3):
                total = total + grecv[g, o, part].astype(jnp.float32)
            kvg[:, pl.ds(pl.multiple_of(part * kv_width + g * HEAD, HEAD), HEAD)] = total.astype(jnp.bfloat16)
        return carry

    lax.fori_loop(0, groups, finish, 0)
    kvg_store = pltpu.make_async_copy(kvg, kvg_hbm, kvg_sem)
    kvg_store.start()

    def drain(g, carry):
        for o in (0, 3):

            @pl.when(exists(o))
            def _():
                far_copy(g, o).wait_send()
                far_grad(g, o).wait_send()

        @pl.when(exists_at(forward))
        def _():
            relay_copy(g).wait_send()

        @pl.when(exists_at(passed))
        def _():
            passed_grad(g).wait_send()

        beside_copy(g).wait_send()
        beside_grad(g).wait_send()
        for copy in store_copies(g):
            copy.wait()
        return carry

    lax.fori_loop(0, groups, drain, 0)
    kvg_store.wait()


def flush(att, dq, kvg, att_out, dq_out, kvg_out, att_held, dq_held, kvg_held, in_sem, out_sem):
    width = kvg.shape[1]
    pieces = []
    for start in range(0, att.shape[1], width):
        pieces.append((att, att_held, att_out, start))
        pieces.append((dq, dq_held, dq_out, start))
    pieces.append((kvg, kvg_held, kvg_out, 0))
    loads = []
    stores = []
    for i, (source, held, result, start) in enumerate(pieces):
        part = pl.ds(start, width)
        loads.append(pltpu.make_async_copy(source.at[:, part], held.at[:, part], in_sem.at[i]))
        stores.append(pltpu.make_async_copy(held.at[:, part], result.at[:, part], out_sem.at[i]))
    for load in loads:
        load.start()
    for load, store in zip(loads, stores):
        load.wait()
        store.start()
    for store in stores:
        store.wait()


def body(queries, keys_values, out_grad, key_blocks, key_count, block_at_slot):
    n = lax.axis_size("ctx")
    rows, width = queries.shape
    kv_width = keys_values.shape[1] // 2
    groups = kv_width // HEAD
    repeats = width // kv_width
    anywhere = pl.BlockSpec(memory_space=pl.ANY)
    scalars = pl.BlockSpec(memory_space=pltpu.SMEM)
    wide = pltpu.VMEM((rows, width), jnp.bfloat16)
    narrow = pltpu.VMEM((rows, 2 * kv_width), jnp.bfloat16)
    ring = pltpu.VMEM((groups, 4, 2, rows, HEAD), jnp.bfloat16)
    dma = pltpu.SemaphoreType.DMA
    shapes = (
        jax.ShapeDtypeStruct((rows, width), jnp.bfloat16),
        jax.ShapeDtypeStruct((rows, width), jnp.bfloat16),
        jax.ShapeDtypeStruct((rows, 2 * kv_width), jnp.bfloat16),
    )
    pieces = 2 * (width // (2 * kv_width)) + 1
    results = pl.pallas_call(
        functools.partial(kernel, n, groups, repeats),
        out_shape=shapes,
        in_specs=[scalars] * 3 + [pl.BlockSpec(memory_space=pltpu.HBM)] * 3,
        out_specs=(anywhere, anywhere, anywhere),
        scratch_shapes=[
            wide, pltpu.VMEM((groups, 2, rows, HEAD), jnp.bfloat16), wide, wide, wide, narrow,
            ring, pltpu.VMEM((groups, 2, rows, HEAD), jnp.float32), ring, ring,
            dma((groups, 2)), dma((groups, 2)), dma((groups, 2)), dma,
            dma((groups, 4)), dma((groups, 4)), dma((groups, 4)), dma((groups, 4)),
        ],
        compiler_params=pltpu.CompilerParams(
            collective_id=0, has_side_effects=True, vmem_limit_bytes=60 * 1024 * 1024
        ),
    )(key_blocks.T, key_count, block_at_slot, queries, keys_values, out_grad)
    return pl.pallas_call(
        flush,
        out_shape=shapes,
        in_specs=[anywhere] * 3,
        out_specs=(pl.BlockSpec(memory_space=pltpu.HBM),) * 3,
        scratch_shapes=[wide, wide, narrow, dma((pieces,)), dma((pieces,))],
        compiler_params=pltpu.CompilerParams(vmem_limit_bytes=60 * 1024 * 1024),
    )(*results)


def solution(mesh):
    sharded = P(("groups", "ctx"), None)
    return jax.shard_map(
        body,
        mesh=mesh,
        in_specs=(sharded, sharded, sharded, P("groups", None), P("groups"), P("groups")),
        out_specs=(sharded, sharded, sharded),
        check_vma=False,
    )
```

```python
import functools

import jax
import jax.numpy as jnp
from jax import lax
from jax.experimental import pallas as pl
from jax.experimental.pallas import tpu as pltpu
from jax.sharding import PartitionSpec as P

HEAD = 128
OFFSETS = (-2, -1, 1, 2)
LOG2E = 1.4426950408889634
NEG = -1e30
NT = (((1,), (1,)), ((), ()))


def kernel(
    n, groups, repeats,
    blocks_ref, count_ref, slot_ref, q_hbm, kv_hbm, do_hbm,
    att_hbm, dq_hbm, kvg_hbm,
    q, kv, do, att, dq, kvg, near, own_grad, gsend, grecv,
    in_sem, kv_sem, out_sem, kvg_sem, near_send, near_recv, grad_send, grad_recv,
):
    rows = q.shape[0]
    wide = repeats * HEAD
    kv_width = groups * HEAD
    scale = HEAD ** (-0.5)
    me = lax.axis_index("ctx")

    def exists(o):
        return jnp.logical_and(me + OFFSETS[o] >= 0, me + OFFSETS[o] < n)

    def exists_at(slot):
        there = me + jnp.where(slot < 2, slot - 2, slot - 1)
        return jnp.logical_and(there >= 0, there < n)

    def target(o):
        return {"ctx": me + OFFSETS[o]}

    def column(g, width):
        return pl.ds(pl.multiple_of(g * width, width), width)

    core = lax.rem(me, 2)
    sibling = {"ctx": me + 1 - 2 * core}
    forward = 3 * (1 - core)
    passed = 1 + core
    beside = 2 - core

    def remote(src, dst, sent, received, device):
        return pltpu.make_async_remote_copy(
            src_ref=src, dst_ref=dst, send_sem=sent, recv_sem=received,
            device_id=device, device_id_type=pl.DeviceIdType.MESH,
        )

    def far_copy(g, o):
        return remote(kv.at[g], near.at[g, 3 - o], near_send.at[g, o], near_recv.at[g, 3 - o], target(o))

    def beside_copy(g):
        return remote(
            kv.at[g], near.at[g, 1 + core], near_send.at[g, 1], near_recv.at[g, 1 + core], sibling
        )

    def relay_copy(g):
        return remote(
            near.at[g, forward], near.at[g, 2 - core], near_send.at[g, 2], near_recv.at[g, 2 - core], sibling
        )

    def near_wait(g, slot):
        remote(
            near.at[g, slot], near.at[g, slot], near_send.at[g, 0], near_recv.at[g, slot], sibling
        ).wait_recv()

    def kv_load(g, part):
        return pltpu.make_async_copy(
            kv_hbm.at[:, pl.ds(part * kv_width + g * HEAD, HEAD)], kv.at[g, part], kv_sem.at[g, part]
        )

    def far_grad(g, o):
        return remote(
            gsend.at[g, o], grecv.at[g, 3 - o], grad_send.at[g, o], grad_recv.at[g, 3 - o], target(o)
        )

    def beside_grad(g):
        return remote(gsend.at[g, beside], grecv.at[g, 1], grad_send.at[g, 1], grad_recv.at[g, 1], sibling)

    def passed_grad(g):
        return remote(gsend.at[g, passed], grecv.at[g, 2], grad_send.at[g, 2], grad_recv.at[g, 2], sibling)

    def relay(g):
        @pl.when(exists_at(forward))
        def _():
            near_wait(g, forward)
            relay_copy(g).start()

    def combine(g):
        @pl.when(exists_at(forward))
        def _():
            passed_grad(g).wait_recv()
            both = gsend[g, forward].astype(jnp.float32) + grecv[g, 2].astype(jnp.float32)
            gsend[g, forward] = both.astype(jnp.bfloat16)

        for o, mine in ((3, 0), (0, 1)):

            @pl.when(jnp.logical_and(exists(o), core == mine))
            def _():
                far_grad(g, o).start()

    def load_copies(g):
        return (
            pltpu.make_async_copy(q_hbm.at[:, column(g, wide)], q.at[:, column(g, wide)], in_sem.at[g, 0]),
            pltpu.make_async_copy(do_hbm.at[:, column(g, wide)], do.at[:, column(g, wide)], in_sem.at[g, 1]),
        )

    def store_copies(g):
        return (
            pltpu.make_async_copy(att.at[:, column(g, wide)], att_hbm.at[:, column(g, wide)], out_sem.at[g, 0]),
            pltpu.make_async_copy(dq.at[:, column(g, wide)], dq_hbm.at[:, column(g, wide)], out_sem.at[g, 1]),
        )

    for g in range(groups):
        for part in range(2):
            kv_load(g, part).start()
    for copy in load_copies(0):
        copy.start()
    barrier = pltpu.get_barrier_semaphore()
    pl.semaphore_signal(barrier, inc=1, device_id=sibling, device_id_type=pl.DeviceIdType.MESH)
    for o in (0, 3):

        @pl.when(exists(o))
        def _():
            pl.semaphore_signal(barrier, inc=1, device_id=target(o), device_id_type=pl.DeviceIdType.MESH)

    for o in range(4):

        @pl.when(jnp.logical_not(exists(o)))
        def _():
            near[:, o] = jnp.zeros((groups, 2, rows, HEAD), near.dtype)
            if o in (0, 3):
                grecv[:, o] = jnp.zeros((groups, 2, rows, HEAD), grecv.dtype)

    pl.semaphore_wait(barrier, 1 + exists(0).astype(jnp.int32) + exists(3).astype(jnp.int32))

    for g in range(groups):
        kv_load(g, 0).wait()
        kv_load(g, 1).wait()
        for o in (3, 0):

            @pl.when(exists(o))
            def _():
                far_copy(g, o).start()

        beside_copy(g).start()
        if g > 0:
            for copy in load_copies(g):
                copy.start()

    own_block = slot_ref[me]
    live_count = count_ref[own_block]
    chosen = []
    bias = []
    for j in (1, 2):
        wanted = blocks_ref[j, own_block]
        hits = []
        for o in range(4):
            there = jnp.clip(me + OFFSETS[o], 0, n - 1)
            hits.append(exists(o) & (slot_ref[there] == wanted) & (live_count > j))
        chosen.append(hits)
        bias.append(jnp.where(hits[0] | hits[1] | hits[2] | hits[3], 0.0, NEG).astype(jnp.float32))

    def pick(g, part, hits):
        value = near[g, 0, part]
        for o in range(1, 4):
            value = jnp.where(hits[o], near[g, o, part], value)
        return value

    def step(g, carry):
        for copy in load_copies(g):
            copy.wait()
        near_wait(g, beside)

        @pl.when(exists_at(3 - forward))
        def _():
            near_wait(g, 3 - forward)

        @pl.when(exists_at(passed))
        def _():
            near_wait(g, passed)

        @pl.when(g > 0)
        def _():
            combine(g - 1)

        own_key = kv[g, 0]
        own_value = kv[g, 1]
        keys = jnp.concatenate([own_key, pick(g, 0, chosen[0]), pick(g, 0, chosen[1])], axis=0)
        values = jnp.concatenate([own_value, pick(g, 1, chosen[0]), pick(g, 1, chosen[1])], axis=0)
        keys_t = keys.T
        values_t = values.T
        key_grad = jnp.zeros((3 * rows, HEAD), jnp.float32)
        value_grad = jnp.zeros((3 * rows, HEAD), jnp.float32)
        for pair in range(repeats // 2):
            starts = [pl.multiple_of(g * wide + (2 * pair + i) * HEAD, HEAD) for i in range(2)]
            q2 = jnp.concatenate([q[:, pl.ds(s, HEAD)] for s in starts], axis=0)
            do2 = jnp.concatenate([do[:, pl.ds(s, HEAD)] for s in starts], axis=0)
            raw = lax.dot_general(keys, q2, NT, preferred_element_type=jnp.float32) * (scale * LOG2E)
            scores = jnp.concatenate(
                [raw[:rows], raw[rows : 2 * rows] + bias[0], raw[2 * rows :] + bias[1]], axis=0
            )
            best = jnp.max(scores, axis=0, keepdims=True)
            weights = jnp.exp2(scores - best)
            total = jnp.sum(weights, axis=0, keepdims=True)
            probs = weights * (1.0 / total)
            rounded = probs.astype(jnp.bfloat16)
            prob_grads = lax.dot_general(values, do2, NT, preferred_element_type=jnp.float32)
            delta = jnp.sum(probs * prob_grads, axis=0, keepdims=True)
            score_grads = (probs * (prob_grads - delta)).astype(jnp.bfloat16)
            mixed = jnp.dot(values_t, rounded, preferred_element_type=jnp.float32)
            query_grad = jnp.dot(keys_t, score_grads, preferred_element_type=jnp.float32) * scale
            mixed = mixed.astype(jnp.bfloat16).T
            query_grad = query_grad.astype(jnp.bfloat16).T
            for i in range(2):
                att[:, pl.ds(starts[i], HEAD)] = mixed[i * rows : (i + 1) * rows]
                dq[:, pl.ds(starts[i], HEAD)] = query_grad[i * rows : (i + 1) * rows]
            if pair == 1:

                @pl.when(g + 1 < groups)
                def _():
                    relay(g + 1)

            key_grad = key_grad + jnp.dot(score_grads, q2, preferred_element_type=jnp.float32)
            value_grad = value_grad + jnp.dot(rounded, do2, preferred_element_type=jnp.float32)
        for part, grad in ((0, key_grad * scale), (1, value_grad)):
            own_grad[g, part] = grad[:rows]
            for o in range(4):
                gsend[g, o, part] = jnp.where(
                    chosen[0][o], grad[rows : 2 * rows], jnp.where(chosen[1][o], grad[2 * rows :], 0.0)
                ).astype(jnp.bfloat16)
        @pl.when(exists_at(passed))
        def _():
            passed_grad(g).start()

        for o, mine in ((3, 1), (0, 0)):

            @pl.when(jnp.logical_and(exists(o), core == mine))
            def _():
                far_grad(g, o).start()

        beside_grad(g).start()
        for copy in store_copies(g):
            copy.start()
        return carry

    relay(0)
    lax.fori_loop(0, groups, step, 0)
    combine(groups - 1)

    def finish(g, carry):
        for o in (0, 3):

            @pl.when(exists(3 - o))
            def _():
                far_grad(g, o).wait_recv()

        beside_grad(g).wait_recv()

        for part in range(2):
            total = own_grad[g, part]
            for o in (0, 1, 3):
                total = total + grecv[g, o, part].astype(jnp.float32)
            kvg[:, pl.ds(pl.multiple_of(part * kv_width + g * HEAD, HEAD), HEAD)] = total.astype(jnp.bfloat16)
        return carry

    lax.fori_loop(0, groups, finish, 0)
    kvg_store = pltpu.make_async_copy(kvg, kvg_hbm, kvg_sem)
    kvg_store.start()

    def drain(g, carry):
        for o in (0, 3):

            @pl.when(exists(o))
            def _():
                far_copy(g, o).wait_send()
                far_grad(g, o).wait_send()

        @pl.when(exists_at(forward))
        def _():
            relay_copy(g).wait_send()

        @pl.when(exists_at(passed))
        def _():
            passed_grad(g).wait_send()

        beside_copy(g).wait_send()
        beside_grad(g).wait_send()
        for copy in store_copies(g):
            copy.wait()
        return carry

    lax.fori_loop(0, groups, drain, 0)
    kvg_store.wait()


def flush(att, dq, kvg, att_out, dq_out, kvg_out, att_held, dq_held, kvg_held, in_sem, out_sem):
    width = kvg.shape[1] // 2
    pieces = []
    for start in range(0, att.shape[1], width):
        pieces.append((att, att_held, att_out, start))
        pieces.append((dq, dq_held, dq_out, start))
    for start in range(0, kvg.shape[1], width):
        pieces.append((kvg, kvg_held, kvg_out, start))
    loads = []
    stores = []
    for i, (source, held, result, start) in enumerate(pieces):
        part = pl.ds(start, width)
        loads.append(pltpu.make_async_copy(source.at[:, part], held.at[:, part], in_sem.at[i]))
        stores.append(pltpu.make_async_copy(held.at[:, part], result.at[:, part], out_sem.at[i]))
    for load in loads:
        load.start()
    for load, store in zip(loads, stores):
        load.wait()
        store.start()
    for store in stores:
        store.wait()


def body(queries, keys_values, out_grad, key_blocks, key_count, block_at_slot):
    n = lax.axis_size("ctx")
    rows, width = queries.shape
    kv_width = keys_values.shape[1] // 2
    groups = kv_width // HEAD
    repeats = width // kv_width
    anywhere = pl.BlockSpec(memory_space=pl.ANY)
    scalars = pl.BlockSpec(memory_space=pltpu.SMEM)
    wide = pltpu.VMEM((rows, width), jnp.bfloat16)
    narrow = pltpu.VMEM((rows, 2 * kv_width), jnp.bfloat16)
    ring = pltpu.VMEM((groups, 4, 2, rows, HEAD), jnp.bfloat16)
    dma = pltpu.SemaphoreType.DMA
    shapes = (
        jax.ShapeDtypeStruct((rows, width), jnp.bfloat16),
        jax.ShapeDtypeStruct((rows, width), jnp.bfloat16),
        jax.ShapeDtypeStruct((rows, 2 * kv_width), jnp.bfloat16),
    )
    pieces = 2 * (width // kv_width) + 2
    results = pl.pallas_call(
        functools.partial(kernel, n, groups, repeats),
        out_shape=shapes,
        in_specs=[scalars] * 3 + [pl.BlockSpec(memory_space=pltpu.HBM)] * 3,
        out_specs=(anywhere, anywhere, anywhere),
        scratch_shapes=[
            wide, pltpu.VMEM((groups, 2, rows, HEAD), jnp.bfloat16), wide, wide, wide, narrow,
            ring, pltpu.VMEM((groups, 2, rows, HEAD), jnp.float32), ring, ring,
            dma((groups, 2)), dma((groups, 2)), dma((groups, 2)), dma,
            dma((groups, 4)), dma((groups, 4)), dma((groups, 4)), dma((groups, 4)),
        ],
        compiler_params=pltpu.CompilerParams(
            collective_id=0, has_side_effects=True, vmem_limit_bytes=60 * 1024 * 1024
        ),
    )(key_blocks.T, key_count, block_at_slot, queries, keys_values, out_grad)
    return pl.pallas_call(
        flush,
        out_shape=shapes,
        in_specs=[anywhere] * 3,
        out_specs=(pl.BlockSpec(memory_space=pltpu.HBM),) * 3,
        scratch_shapes=[wide, wide, narrow, dma((pieces,)), dma((pieces,))],
        compiler_params=pltpu.CompilerParams(vmem_limit_bytes=60 * 1024 * 1024),
    )(*results)


def solution(mesh):
    sharded = P(("groups", "ctx"), None)
    return jax.shard_map(
        body,
        mesh=mesh,
        in_specs=(sharded, sharded, sharded, P("groups", None), P("groups"), P("groups")),
        out_specs=(sharded, sharded, sharded),
        check_vma=False,
    )
```
